32 devices in a mesh: groups: 2 (over y), tensor: 8 (over z, x), dp: 2 (over core).
Axes of the slice: x: 2, y: 2, z: 4, core: 2. Of those that a mesh axis runs over, the one named last changes fastest.
Arguments:
- tokens: bfloat16 [2048, 4096], P(('groups', 'tensor', 'dp')), parts along dimension 0, may hold values from -6 to 6
- norm_gain: float32 [4096], replicated, may hold values from 0.5 to 1.5
- gate_codes: bfloat16 [4096, 28672], P(None, 'tensor'), may hold values from -127 to 127, as said below
- gate_scales: float32 [32, 28672], P(None, 'tensor'), may hold values from 0.00010625 to 0.000421875
- up_codes: bfloat16 [4096, 28672], P(None, 'tensor'), may hold values from -127 to 127, as said below
- up_scales: float32 [32, 28672], P(None, 'tensor'), may hold values from 0.00010625 to 0.000421875
- down_codes: bfloat16 [28672, 4096], P('tensor'), may hold values from -127 to 127, as said below
- down_scales: float32 [1024, 4096], P('tensor'), may hold values from 4.0158724e-05 to 0.00015945376
Outputs:
- layer_out: bfloat16 [2048, 4096], P(('groups', 'tensor', 'dp')), parts along dimension 0
The draws below stay inside these ranges and needn't reach their ends.
There are 2 independent parts, one for each index of `groups`. The reference program is written for one: setup_inputs(seed, part) draws one part's arguments, and reference() takes and returns one part's arrays. A program takes and returns all parts, laid end to end along the dimension named above; an argument that names none is the same for every part. Nothing has to cross between parts.
Inputs may be any that keep to these rules, and one draw needn't show every extreme that they name: `gate_codes`: every entry is a whole number. `up_codes`: every entry is a whole number. `down_codes`: every entry is a whole number.
All inputs are finite; a program needn't handle non-finite values.
Results may differ from the reference program's by a relative error of at most 0.012.
Values may be sent and summed in bfloat16 or wider, within the bound.
A program may use at most 320 MiB of HBM per device.

```python
import math
import jax
import jax.numpy as jnp
from jax import lax

D = 4096
WALSH = 1024
HB = 28
QBLOCK = 128
FF = 28672
TOKENS = 1024


def draw_gate_codes(key, part):
    return jax.random.randint(jax.random.fold_in(key, 11), (D, FF), -127, 128).astype(jnp.bfloat16)


def draw_up_codes(key, part):
    return jax.random.randint(jax.random.fold_in(key, 23), (D, FF), -127, 128).astype(jnp.bfloat16)


def draw_down_codes(key, part):
    return jax.random.randint(jax.random.fold_in(key, 37), (FF, D), -127, 128).astype(jnp.bfloat16)


def steps_of(stream_key, shape, cuts, smallest, high):
    gain, own = 1.0, jax.random.fold_in(stream_key, 6)
    for axis_at, blocks in cuts:
        draws = jnp.exp(jax.random.uniform(jax.random.fold_in(own, axis_at), (blocks,), jnp.float32, smallest / len(cuts), high / len(cuts)))
        gain = gain * jnp.repeat(draws, shape[axis_at] // blocks).reshape([-1 if axis == axis_at else 1 for axis in range(len(shape))])
    return gain


def centred(key, shape, scale, bound, pieces=(), kind=jnp.bfloat16):
    loudness = steps_of(key, shape, pieces, -0.22, 0.18) if pieces else 1.0
    result = jax.random.normal(key, shape, jnp.float32) * scale * loudness
    return jnp.minimum(jnp.maximum(result, -bound), bound).astype(kind)


def setup_inputs(seed: int = 0, part: int = 0) -> dict:
    arg_keys = jax.random.split(jax.random.key(seed), 9)
    part_splits = jax.random.split(jax.random.fold_in(arg_keys[8], part), 9)
    return {
        "tokens": centred(part_splits[0], (TOKENS, D), 1.0, 6.0, ((0, 16),)),
        "norm_gain": jnp.clip(1.0 + 0.1 * jax.random.normal(arg_keys[1], (D,), jnp.float32), 0.5, 1.5),
        "gate_codes": draw_gate_codes(jax.random.fold_in(arg_keys[8], 71), part),
        "gate_scales": jnp.clip(jnp.exp(math.log(0.000421875) - 1.37891427 * jax.random.uniform(arg_keys[3], (D // QBLOCK, FF), jnp.float32) ** steps_of(arg_keys[3], (D // QBLOCK, FF), ((1, 8),), -0.2, 0.2)), 0.00010625, 0.000421875),
        "up_codes": draw_up_codes(jax.random.fold_in(arg_keys[8], 71), part),
        "up_scales": jnp.clip(jnp.exp(math.log(0.000421875) - 1.37891427 * jax.random.uniform(arg_keys[5], (D // QBLOCK, FF), jnp.float32) ** steps_of(arg_keys[5], (D // QBLOCK, FF), ((1, 8),), -0.2, 0.2)), 0.00010625, 0.000421875),
        "down_codes": draw_down_codes(jax.random.fold_in(arg_keys[8], 71), part),
        "down_scales": jnp.clip(jnp.exp(math.log(0.00015945376) - 1.37891428 * jax.random.uniform(arg_keys[7], (WALSH, D), jnp.float32) ** steps_of(arg_keys[7], (WALSH, D), ((0, 8),), -0.2, 0.2)), 4.015872400486842e-05, 0.00015945376),
    }


EPSILON = 1e-05

def hadamard_small():
    modulus = 13
    residues = [number * number % modulus for number in range(1, modulus)]
    legendre = [0] + [1 if number in residues else -1 for number in range(1, modulus)]
    plus_block = [[1, 1], [1, -1]]
    zero_block = [[1, -1], [-1, -1]]

    def conference_entry(row_number, column_number):
        if row_number == 0 and column_number == 0:
            return 0
        if row_number == 0 or column_number == 0:
            return 1
        return legendre[(column_number - row_number) % modulus]
    table = [[conference_entry(row_block, column_block) * plus_block[row_inner][column_inner] + (zero_block[row_inner][column_inner] if row_block == column_block else 0) for column_block in range(modulus + 1) for column_inner in range(2)] for row_block in range(modulus + 1) for row_inner in range(2)]
    return jnp.asarray(table, jnp.float32)

def walsh(order):
    counter = jnp.arange(order, dtype=jnp.int32)
    common = counter[:, None] & counter[None, :]
    parity = jnp.zeros((order, order), jnp.int32)
    for level in range(order.bit_length() - 1):
        parity = parity + (common >> level & 1)
    return (1 - 2 * (parity % 2)).astype(jnp.float32)

def dequantize(codes, scales):
    blocks = scales.shape[0]
    height = codes.shape[0]
    width = codes.shape[1]
    spread = codes.astype(jnp.float32).reshape(blocks, height // blocks, width) * scales[:, None, :]
    return spread.reshape(height, width).astype(jnp.bfloat16)

def rotate(hidden):
    height = hidden.shape[0]
    blocks = hidden.astype(jnp.float32).reshape(height, WALSH, HB)
    small_table = hadamard_small()
    blocks = jnp.einsum('tia,ac->tic', blocks, small_table, precision=lax.Precision.HIGHEST)
    blocks = jnp.einsum('ji,tic->tjc', walsh(WALSH), blocks, precision=lax.Precision.HIGHEST)
    return (blocks * FF ** (-0.5)).reshape(height, FF).astype(jnp.bfloat16)

def reference(tokens, norm_gain, gate_codes, gate_scales, up_codes, up_scales, down_codes, down_scales):
    floated = tokens.astype(jnp.float32)
    normed = (floated * lax.rsqrt(lax.optimization_barrier(jnp.mean(floated * floated, axis=1, keepdims=True)) + EPSILON) * norm_gain).astype(jnp.bfloat16)
    gate_weight = dequantize(gate_codes, gate_scales)
    up_weight = dequantize(up_codes, up_scales)
    down_weight = dequantize(down_codes, down_scales)
    gate = jnp.dot(normed, gate_weight, preferred_element_type=jnp.float32)
    upward = jnp.dot(normed, up_weight, preferred_element_type=jnp.float32)
    hidden = (jax.nn.silu(gate) * upward).astype(jnp.bfloat16)
    rotated = rotate(hidden)
    down = jnp.dot(rotated, down_weight, preferred_element_type=jnp.float32)
    return (floated + down).astype(jnp.bfloat16)
```

```python
import math

import jax
import jax.numpy as jnp
import numpy as np
from jax import lax
from jax.experimental import pallas as pl
from jax.sharding import PartitionSpec as P

HB = 28
EPSILON = 1e-05
LANES = 128
SUBLANES = 8
PACKED_ROWS = 16
HALVES = 2


def from_partner(value, axis, stride):
    return lax.ppermute(value, axis, [(i, i ^ 1 << stride) for i in range(lax.axis_size(axis))])


def hadamard_small():
    modulus = 13
    residues = [number * number % modulus for number in range(1, modulus)]
    legendre = [0] + [1 if number in residues else -1 for number in range(1, modulus)]
    conference = np.ones((modulus + 1, modulus + 1))
    conference[0, 0] = 0
    for row in range(modulus):
        for column in range(modulus):
            conference[row + 1, column + 1] = legendre[(column - row) % modulus]
    return np.kron(conference, [[1, 1], [1, -1]]) + np.kron(
        np.eye(modulus + 1), [[1, -1], [-1, -1]]
    )


def walsh(order):
    table = np.ones((1, 1))
    while table.shape[0] < order:
        table = np.kron([[1, 1], [1, -1]], table)
    return table


def dequantize(codes, scales):
    blocks = scales.shape[0]
    height, width = codes.shape
    spread = codes.astype(jnp.float32).reshape(blocks, height // blocks, width) * scales[:, None, :]
    return spread.reshape(height, width).astype(jnp.bfloat16)


def down_body(span, codes_ref, scales_ref, out_ref):
    height, width = codes_ref.shape
    row = lax.broadcasted_iota(jnp.int32, (PACKED_ROWS, width), 0)
    for start in range(0, height, PACKED_ROWS):
        first, last = start // span, (start + PACKED_ROWS - 1) // span
        scale = scales_ref[first : first + 1, :]
        if last != first:
            scale = jnp.where(row < last * span - start, scale, scales_ref[last : last + 1, :])
        rows = slice(start, start + PACKED_ROWS)
        out_ref[rows, :] = (codes_ref[rows, :].astype(jnp.float32) * scale).astype(jnp.bfloat16)


def dequantize_down(codes, scales):
    height, width = codes.shape
    span = height // scales.shape[0]
    tall, wide = SUBLANES * span, min(width, 2048)
    return pl.pallas_call(
        lambda *refs: down_body(span, *refs),
        grid=(height // tall, width // wide),
        in_specs=[
            pl.BlockSpec((tall, wide), lambda r, c: (r, c)),
            pl.BlockSpec((SUBLANES, wide), lambda r, c: (r, c)),
        ],
        out_specs=pl.BlockSpec((tall, wide), lambda r, c: (r, c)),
        out_shape=jax.ShapeDtypeStruct((height, width), jnp.bfloat16),
        cost_estimate=pl.CostEstimate(
            flops=height * width, bytes_accessed=4 * height * width, transcendentals=0
        ),
    )(codes, scales)


def gather(block, levels, position):
    blocks = block[None]
    for level in reversed(range(levels)):
        partner = from_partner(blocks, "tensor", level)
        upper = (position >> level & 1) == 1
        low = jnp.where(upper, partner, blocks)
        high = jnp.where(upper, blocks, partner)
        blocks = jnp.stack([low, high], axis=1).reshape(-1, *block.shape)
    return blocks.reshape(-1, block.shape[1])


def scatter(total, levels, position):
    blocks = total.reshape(1 << levels, -1, total.shape[1])
    for level in range(levels):
        bit = position >> level & 1
        pairs = blocks.reshape(-1, 2, *blocks.shape[1:])
        kept = lax.dynamic_index_in_dim(pairs, bit, 1, keepdims=False)
        sent = lax.dynamic_index_in_dim(pairs, 1 - bit, 1, keepdims=False)
        partner = from_partner(sent, "tensor", level)
        blocks = (kept.astype(jnp.float32) + partner.astype(jnp.float32)).astype(jnp.bfloat16)
    return blocks[0]


def shards(
    tokens, norm_gain, gate_codes, gate_scales, up_codes, up_scales, down_codes, down_scales
):
    devices = lax.axis_size("tensor")
    levels = devices.bit_length() - 1
    position = lax.axis_index("tensor")
    local_width = gate_codes.shape[1]
    local_walsh = local_width // HB
    hidden_units = local_width * devices
    inner_walsh = min(local_walsh, LANES // math.gcd(HB, LANES))
    slab = inner_walsh * HB
    slabs = local_walsh // inner_walsh
    inner_table = jnp.asarray(np.kron(walsh(inner_walsh), hadamard_small()), jnp.bfloat16)

    floated = tokens.astype(jnp.float32)
    normed = (
        floated
        * lax.rsqrt(jnp.mean(floated * floated, axis=1, keepdims=True) + EPSILON)
        * norm_gain
    ).astype(jnp.bfloat16)
    part = tokens.shape[0] // HALVES
    gathered = [
        gather(normed[half * part : (half + 1) * part], levels, position)
        for half in range(HALVES)
    ]
    weights = []
    for number in range(slabs):
        columns = slice(number * slab, (number + 1) * slab)
        weights.append(
            (
                dequantize(gate_codes[:, columns], gate_scales[:, columns]),
                dequantize(up_codes[:, columns], up_scales[:, columns]),
            )
        )

    pieces = []
    for half in range(HALVES):
        rows = gathered[half]
        if half:
            rows, pieces[-1] = lax.optimization_barrier((rows, pieces[-1]))
        for gate_weight, up_weight in weights:
            gate = jnp.dot(rows, gate_weight, preferred_element_type=jnp.float32)
            upward = jnp.dot(rows, up_weight, preferred_element_type=jnp.float32)
            pieces.append((jax.nn.silu(gate) * upward).astype(jnp.bfloat16))
    down_codes, pieces[-1] = lax.optimization_barrier((down_codes, pieces[-1]))
    down_weight = dequantize_down(down_codes, down_scales)

    order = list(reversed(range(levels)))
    partners = [from_partner(piece, "tensor", order[0]) for piece in pieces]
    count = len(pieces)
    for step in range(count + levels - 1):
        active = [
            (step - stage, stage) for stage in range(levels) if 0 <= step - stage < count
        ]
        for index, stage in active:
            sign = (1 - 2 * (position >> order[stage] & 1)).astype(jnp.float32)
            pieces[index] = (
                partners[index].astype(jnp.float32) + sign * pieces[index].astype(jnp.float32)
            ).astype(jnp.bfloat16)
            if stage + 1 < levels:
                partners[index] = from_partner(pieces[index], "tensor", order[stage + 1])
        tied = sorted(
            {index for index, stage in active if stage + 1 < levels}
            | ({step + 1} if step + 1 < count else set())
        )
        tied += [index for index, stage in active if stage + 1 == levels]
        fixed = lax.optimization_barrier(tuple(pieces[index] for index in tied))
        for index, value in zip(tied, fixed):
            pieces[index] = value

    outputs = []
    for half in range(HALVES):
        mixed = [
            jnp.dot(piece, inner_table, preferred_element_type=jnp.float32)
            for piece in pieces[half * slabs : (half + 1) * slabs]
        ]
        stride = 1
        while stride < slabs:
            mixed = [
                mixed[index] + mixed[index ^ stride]
                if not index & stride
                else mixed[index ^ stride] - mixed[index]
                for index in range(slabs)
            ]
            stride *= 2
        rotated = jnp.concatenate(
            [(piece * hidden_units ** (-0.5)).astype(jnp.bfloat16) for piece in mixed], axis=1
        )
        down = jnp.dot(rotated, down_weight, preferred_element_type=jnp.float32)
        summed = scatter(down.astype(jnp.bfloat16), levels, position)
        outputs.append(
            (floated[half * part : (half + 1) * part] + summed.astype(jnp.float32)).astype(
                jnp.bfloat16
            )
        )
    return jnp.concatenate(outputs, axis=0)


def solution(mesh):
    return jax.shard_map(
        shards,
        mesh=mesh,
        in_specs=(
            P(("groups", "tensor", "dp"), None),
            P(),
            P(None, "tensor"),
            P(None, "tensor"),
            P(None, "tensor"),
            P(None, "tensor"),
            P("tensor", None),
            P("tensor", None),
        ),
        out_specs=P(("groups", "tensor", "dp"), None),
        check_vma=False,
    )
```
